32 devices in a mesh: dp: 8 (over y, x, core), tensor: 4 (over z).
Axes of the slice: x: 2, y: 2, z: 4, core: 2. Of those that a mesh axis runs over, the one named last changes fastest.
Arguments:
- tokens: bfloat16 [4096, 1024], P(('dp', 'tensor')), may hold values from -6 to 6
- seg_ids: int32 [8, 512], P('dp'), may hold values from 0 to 3, never falling along the last dimension, each value on 1 to 256 neighbouring positions
- attn_gain: float32 [1024], replicated, may hold values from 0.5 to 1.5
- w_query: bfloat16 [1024, 1024], P(None, 'tensor'), may hold values from -0.1875 to 0.1875
- w_key: bfloat16 [1024, 1024], P(None, 'tensor'), may hold values from -0.1875 to 0.1875
- w_value: bfloat16 [1024, 2048], P(None, 'tensor'), may hold values from -0.1875 to 0.1875
- w_gate: bfloat16 [1024, 2048], P(None, 'tensor'), may hold values from -0.1875 to 0.1875
- w_decay: bfloat16 [1024, 8], P(None, 'tensor'), may hold values from -0.1875 to 0.1875
- w_beta: bfloat16 [1024, 8], P(None, 'tensor'), may hold values from -0.1875 to 0.1875
- conv_query: float32 [4, 1024], P(None, 'tensor'), may hold values from -3 to 3
- conv_key: float32 [4, 1024], P(None, 'tensor'), may hold values from -3 to 3
- conv_value: float32 [4, 2048], P(None, 'tensor'), may hold values from -3 to 3
- decay_rate: float32 [8], P('tensor'), may hold values from 0.005 to 1
- out_gain: float32 [256], replicated, may hold values from 0.5 to 1.5
- w_out: bfloat16 [2048, 1024], P('tensor'), may hold values from -0.25 to 0.25
- ffn_gain: float32 [1024], replicated, may hold values from 0.5 to 1.5
- w_ffn_gate: bfloat16 [1024, 2816], P(None, 'tensor'), may hold values from -0.1875 to 0.1875
- w_ffn_up: bfloat16 [1024, 2816], P(None, 'tensor'), may hold values from -0.1875 to 0.1875
- w_ffn_down: bfloat16 [2816, 1024], P('tensor'), may hold values from -0.21875 to 0.21875
- grad_out: bfloat16 [4096, 1024], P(('dp', 'tensor')), may hold values from -6 to 6
Outputs:
- block_out: bfloat16 [4096, 1024], P(('dp', 'tensor'))
- grad_tokens: bfloat16 [4096, 1024], P(('dp', 'tensor'))
- grad_attn_gain: float32 [1024], replicated
- grad_w_query: float32 [1024, 1024], P('dp', 'tensor')
- grad_w_key: float32 [1024, 1024], P('dp', 'tensor')
- grad_w_value: float32 [1024, 2048], P('dp', 'tensor')
- grad_w_gate: float32 [1024, 2048], P('dp', 'tensor')
- grad_w_decay: float32 [1024, 8], P('dp', 'tensor')
- grad_w_beta: float32 [1024, 8], P('dp', 'tensor')
- grad_conv_query: float32 [4, 1024], P(None, 'tensor')
- grad_conv_key: float32 [4, 1024], P(None, 'tensor')
- grad_conv_value: float32 [4, 2048], P(None, 'tensor')
- grad_decay_rate: float32 [8], P('tensor')
- grad_out_gain: float32 [256], replicated
- grad_w_out: float32 [2048, 1024], P('tensor', 'dp')
- grad_ffn_gain: float32 [1024], replicated
- grad_w_ffn_gate: float32 [1024, 2816], P('dp', 'tensor')
- grad_w_ffn_up: float32 [1024, 2816], P('dp', 'tensor')
- grad_w_ffn_down: float32 [2816, 1024], P('tensor', 'dp')
The draws below stay inside these ranges and needn't reach their ends.
Inputs may be any that keep to these rules, and one draw needn't show every extreme that they name: `seg_ids`: along each sequence the document numbers never fall; each document has 1 to 256 tokens.
All inputs are finite; a program needn't handle non-finite values.
Results may differ from the reference program's by a relative error of at most 0.018.
Values may be sent and summed in bfloat16 or wider, within the bound.
A program may use at most 192 MiB of HBM per device.

```python
import math
from functools import partial
import jax
import jax.numpy as jnp
import numpy as np
from jax import lax

D = 1024
HEADS = 8
KEY_DIM = 128
VAL_DIM = 256
FF = 2816
CONV = 4
GROUP = 64
LEN = 512
SEQS = 8
TOKENS = 4096


def steps_of(stream_key, extent, pieces, low, largest):
    def one(dim, blocks):
        heights = jax.random.uniform(jax.random.fold_in(jax.random.fold_in(stream_key, 6), dim), (blocks,), jnp.float32, low / len(pieces), largest / len(pieces))
        return jnp.repeat(jnp.exp(heights), extent[dim] // blocks).reshape((-1,) + (1,) * (len(extent) - dim - 1))

    level = one(*pieces[0])
    for cut in pieces[1:]:
        level = level * one(*cut)
    return level


def split_up(amount, total, reach, slope):
    weights = [(1 << 20) // math.isqrt(grade ** slope) + 1 for grade in range(2, amount + 1)]
    spare, holding = total - reach - (amount - 1), [1] * (amount - 1)
    while spare > 0:
        candidates = [i for i in range(amount - 1) if holding[i] < reach]
        whole, budget = sum([weights[i] for i in candidates]), spare
        for i in candidates:
            more = min(reach - holding[i], max(1, budget * weights[i] // whole), spare)
            holding[i] = holding[i] + more
            spare = spare - more
    return np.array([reach] + holding)


def uneven_parts(own_key, number_of, total, bound, lean):
    if number_of == 2:
        one = jax.random.randint(own_key, (), max(1, total - bound), min(bound, total - 1) + 1)
        return jnp.stack([one, total - one])
    sizes = jnp.asarray(split_up(number_of, total, bound, lean), jnp.int32)
    pairs = (number_of - 1) // 2
    donor, taker = sizes[1:1 + 2 * pairs:2], sizes[2:2 + 2 * pairs:2]
    room = jnp.minimum(donor - 1, bound - taker)
    shifted = jax.random.randint(jax.random.fold_in(own_key, 1), (pairs,), 0, 1 << 20) % (room + 1)
    sizes = sizes.at[1:1 + 2 * pairs:2].set(donor - shifted).at[2:2 + 2 * pairs:2].set(taker + shifted)
    return sizes[jax.random.permutation(jax.random.fold_in(own_key, 2), number_of)]


def gaussian(stream_key, dims, scale, bound, cuts=(), held_as=jnp.bfloat16):
    drawn = jax.random.normal(stream_key, dims, jnp.float32) * scale
    if len(cuts) > 0:
        drawn = steps_of(stream_key, dims, cuts, -0.22, 0.18) * drawn
    return jnp.clip(drawn, min=-bound, max=bound).astype(held_as)


def setup_inputs(seed: int = 0) -> dict:
    arg_keys = jax.random.split(jax.random.key(seed), 21)
    return {
        "tokens": gaussian(arg_keys[0], (TOKENS, D), 1.0, 6.0, ((0, 32),)),
        "seg_ids": jax.vmap(lambda own: jnp.searchsorted(jnp.cumsum(uneven_parts(own, 4, LEN, LEN // 2, 1)), jnp.arange(LEN), side="right"))(jax.random.split(arg_keys[1], SEQS)).reshape((SEQS, LEN)).astype(jnp.int32),
        "attn_gain": jnp.clip(1.0 + 0.1 * jax.random.normal(arg_keys[2], (D,), jnp.float32), 0.5, 1.5),
        "w_query": gaussian(arg_keys[3], (D, HEADS * KEY_DIM), D ** -0.5, 0.1875, ((1, 4),)),
        "w_key": gaussian(arg_keys[4], (D, HEADS * KEY_DIM), D ** -0.5, 0.1875, ((1, 4),)),
        "w_value": gaussian(arg_keys[5], (D, HEADS * VAL_DIM), D ** -0.5, 0.1875, ((1, 4),)),
        "w_gate": gaussian(arg_keys[6], (D, HEADS * VAL_DIM), D ** -0.5, 0.1875, ((1, 4),)),
        "w_decay": gaussian(arg_keys[7], (D, HEADS), D ** -0.5, 0.1875, ((1, 4),)),
        "w_beta": gaussian(arg_keys[8], (D, HEADS), D ** -0.5, 0.1875, ((1, 4),)),
        "conv_query": gaussian(arg_keys[9], (CONV, HEADS * KEY_DIM), CONV ** -0.5, 3.0, ((1, 4),), jnp.float32),
        "conv_key": gaussian(arg_keys[10], (CONV, HEADS * KEY_DIM), CONV ** -0.5, 3.0, ((1, 4),), jnp.float32),
        "conv_value": gaussian(arg_keys[11], (CONV, HEADS * VAL_DIM), CONV ** -0.5, 3.0, ((1, 4),), jnp.float32),
        "decay_rate": jnp.clip(jnp.exp(math.log(1.0) - 5.2983174 * jax.random.uniform(arg_keys[12], (HEADS,), jnp.float32) ** steps_of(arg_keys[12], (HEADS,), ((0, 4),), -0.2, 0.2)), 0.005, 1.0),
        "out_gain": jnp.clip(1.0 + 0.1 * jax.random.normal(arg_keys[13], (VAL_DIM,), jnp.float32), 0.5, 1.5),
        "w_out": gaussian(arg_keys[14], (HEADS * VAL_DIM, D), (HEADS * VAL_DIM // 4) ** -0.5, 0.25, ((0, 4),)),
        "ffn_gain": jnp.clip(1.0 + 0.1 * jax.random.normal(arg_keys[15], (D,), jnp.float32), 0.5, 1.5),
        "w_ffn_gate": gaussian(arg_keys[16], (D, FF), D ** -0.5, 0.1875, ((1, 4),)),
        "w_ffn_up": gaussian(arg_keys[17], (D, FF), D ** -0.5, 0.1875, ((1, 4),)),
        "w_ffn_down": gaussian(arg_keys[18], (FF, D), (FF // 4) ** -0.5, 0.21875, ((0, 4),)),
        "grad_out": gaussian(arg_keys[19], (TOKENS, D), 1.0, 6.0, ((0, 32),)),
    }


EPS_NORM = 1e-05
EPS_UNIT = 1e-06
HIGH = lax.Precision.HIGHEST

def norm_gain(values, gain):
    return values * lax.rsqrt(lax.optimization_barrier(jnp.mean(values * values, axis=-1, keepdims=True)) + EPS_NORM) * gain

def shift_rows(values, offset, fill):
    padding = jnp.full((offset,) + values.shape[1:], fill, values.dtype)
    return jnp.concatenate([padding, values[:-offset]], axis=0)

def short_conv(values, taps, seg_row):
    total = taps[0] * values
    for offset in range(1, taps.shape[0]):
        keep = (seg_row == shift_rows(seg_row, offset, -1)).astype(values.dtype)
        total = total + taps[offset] * shift_rows(values, offset, 0) * keep[:, None]
    return total

def unit_rows(values):
    return values * lax.rsqrt(lax.optimization_barrier(jnp.sum(values * values, axis=-1, keepdims=True)) + EPS_UNIT)

def delta_block(carry, block):
    state, prev_doc = carry
    query, keys, values, beta, log_decay, doc = block
    size = doc.shape[0]
    index = jnp.arange(size)
    lower = index[:, None] >= index[None, :]
    strict = (index[:, None] > index[None, :]).astype(state.dtype)
    same_doc = ((doc[:, None] == doc[None, :]) & lower).astype(state.dtype)
    cum_log = jnp.cumsum(log_decay, axis=0).T
    spread = jnp.exp(jnp.minimum(cum_log[:, :, None] - cum_log[:, None, :], 0.0)) * same_doc[None]
    carried_keep = jnp.exp(cum_log) * (doc == prev_doc).astype(state.dtype)[None, :]
    key_key = jnp.einsum('thd,ihd->hti', keys, keys, precision=HIGH)
    beta_rows = beta.T[:, :, None]
    system = jnp.eye(size, dtype=state.dtype)[None] + beta_rows * key_key * spread * strict[None]
    from_state = jnp.einsum('thd,hde->hte', keys, state, precision=HIGH)
    right_side = beta_rows * (jnp.transpose(values, (1, 0, 2)) - carried_keep[:, :, None] * from_state)
    delta = lax.linalg.triangular_solve(system, right_side, left_side=True, lower=True, unit_diagonal=True)
    query_key = jnp.einsum('thd,ihd->hti', query, keys, precision=HIGH)
    mixed = jnp.einsum('hti,hie->the', query_key * spread, delta, precision=HIGH)
    mixed = mixed + jnp.einsum('thd,hde->the', query * carried_keep.T[:, :, None], state, precision=HIGH)
    final_row = spread[:, -1, :]
    new_state = carried_keep[:, -1][:, None, None] * state + jnp.einsum('ihd,hi,hie->hde', keys, final_row, delta, precision=HIGH)
    return ((new_state, doc[-1]), mixed)

def mixer(seg_row, q_proj, k_proj, v_proj, gate_proj, decay_proj, beta_proj, conv_query, conv_key, conv_value, decay_rate, out_gain):
    length = q_proj.shape[0]
    heads = decay_proj.shape[1]
    key_dim = q_proj.shape[1] // heads
    val_dim = v_proj.shape[1] // heads
    query = unit_rows(jax.nn.silu(short_conv(q_proj, conv_query, seg_row)).reshape(length, heads, key_dim)) / math.sqrt(key_dim)
    keys = unit_rows(jax.nn.silu(short_conv(k_proj, conv_key, seg_row)).reshape(length, heads, key_dim))
    values = jax.nn.silu(short_conv(v_proj, conv_value, seg_row)).reshape(length, heads, val_dim)
    beta = jax.nn.sigmoid(beta_proj)
    log_decay = -decay_rate[None, :] * jax.nn.softplus(decay_proj)
    blocks = length // GROUP

    def split(array):
        return array.reshape((blocks, GROUP) + array.shape[1:])
    init = (jnp.zeros((heads, key_dim, val_dim), q_proj.dtype), jnp.array(-1, dtype=seg_row.dtype))
    _, mixed = lax.scan(delta_block, init, (split(query), split(keys), split(values), split(beta), split(log_decay), split(seg_row)))
    mixed = mixed.reshape(length, heads, val_dim)
    gate = gate_proj.reshape(length, heads, val_dim)
    normed = mixed * lax.rsqrt(lax.optimization_barrier(jnp.mean(mixed * mixed, axis=-1, keepdims=True)) + EPS_NORM) * out_gain * jax.nn.silu(gate)
    return normed.reshape(length, heads * val_dim)

def reference(tokens, seg_ids, attn_gain, w_query, w_key, w_value, w_gate, w_decay, w_beta, conv_query, conv_key, conv_value, decay_rate, out_gain, w_out, ffn_gain, w_ffn_gate, w_ffn_up, w_ffn_down, grad_out):
    seq_count = seg_ids.shape[0]
    length = seg_ids.shape[1]
    width = tokens.shape[1]
    token_seqs = tokens.reshape(seq_count, length, width)
    grad_seqs = grad_out.reshape(seq_count, length, width)
    mats = (w_query, w_key, w_value, w_gate, w_decay, w_beta)
    params = (conv_query, conv_key, conv_value, decay_rate, out_gain)

    def one_seq(carry, item):
        x_seq, dy_seq, seg_row = item
        x_float = x_seq.astype(jnp.float32)
        xnorm = norm_gain(x_float, attn_gain).astype(jnp.bfloat16)
        projs = [jnp.dot(xnorm.astype(jnp.float32), weight.astype(jnp.float32), preferred_element_type=jnp.float32) for weight in mats]
        mixed, pull_mix = jax.vjp(partial(mixer, seg_row), projs[0], projs[1], projs[2], projs[3], projs[4], projs[5], params[0], params[1], params[2], params[3], params[4])
        gated = mixed.astype(jnp.bfloat16)
        resid = x_float + jnp.dot(gated.astype(jnp.float32), w_out.astype(jnp.float32), preferred_element_type=jnp.float32)
        hnorm = norm_gain(resid, ffn_gain).astype(jnp.bfloat16)
        up_in = jnp.dot(hnorm.astype(jnp.float32), w_ffn_gate.astype(jnp.float32), preferred_element_type=jnp.float32)
        up_val = jnp.dot(hnorm.astype(jnp.float32), w_ffn_up.astype(jnp.float32), preferred_element_type=jnp.float32)
        act = (jax.nn.silu(up_in) * up_val).astype(jnp.bfloat16)
        out_seq = (resid + jnp.dot(act.astype(jnp.float32), w_ffn_down.astype(jnp.float32), preferred_element_type=jnp.float32)).astype(jnp.bfloat16)
        d_act = jnp.dot(dy_seq.astype(jnp.float32), w_ffn_down.T.astype(jnp.float32), preferred_element_type=jnp.float32)
        g_down = jnp.dot(act.T.astype(jnp.float32), dy_seq.astype(jnp.float32), preferred_element_type=jnp.float32)
        gate_sig = jax.nn.sigmoid(up_in)
        d_up_in = (d_act * up_val * gate_sig * (1.0 + up_in * (1.0 - gate_sig))).astype(jnp.bfloat16)
        d_up_val = (d_act * up_in * gate_sig).astype(jnp.bfloat16)
        g_fgate = jnp.dot(hnorm.T.astype(jnp.float32), d_up_in.astype(jnp.float32), preferred_element_type=jnp.float32)
        g_fup = jnp.dot(hnorm.T.astype(jnp.float32), d_up_val.astype(jnp.float32), preferred_element_type=jnp.float32)
        d_hnorm = jnp.dot(d_up_in.astype(jnp.float32), w_ffn_gate.T.astype(jnp.float32), preferred_element_type=jnp.float32) + jnp.dot(d_up_val.astype(jnp.float32), w_ffn_up.T.astype(jnp.float32), preferred_element_type=jnp.float32)
        _, pull_mid = jax.vjp(norm_gain, resid, ffn_gain)
        d_resid_norm, g_fgain = pull_mid(d_hnorm)
        d_resid = dy_seq.astype(jnp.float32) + d_resid_norm
        d_resid_b = d_resid.astype(jnp.bfloat16)
        g_out = jnp.dot(gated.T.astype(jnp.float32), d_resid_b.astype(jnp.float32), preferred_element_type=jnp.float32)
        d_gated = jnp.dot(d_resid_b.astype(jnp.float32), w_out.T.astype(jnp.float32), preferred_element_type=jnp.float32)
        back = pull_mix(d_gated)
        d_projs = [grad.astype(jnp.bfloat16) for grad in back[:6]]
        g_mats = [jnp.dot(xnorm.T.astype(jnp.float32), grad.astype(jnp.float32), preferred_element_type=jnp.float32) for grad in d_projs]
        d_xnorm = jnp.dot(d_projs[0].astype(jnp.float32), mats[0].T.astype(jnp.float32), preferred_element_type=jnp.float32)
        for grad, weight in zip(d_projs[1:], mats[1:]):
            d_xnorm = d_xnorm + jnp.dot(grad.astype(jnp.float32), weight.T.astype(jnp.float32), preferred_element_type=jnp.float32)
        _, pull_first = jax.vjp(norm_gain, x_float, attn_gain)
        d_x_norm, g_again = pull_first(d_xnorm)
        dx_seq = (d_resid + d_x_norm).astype(jnp.bfloat16)
        grads = (g_again,) + tuple(g_mats) + tuple(back[6:10]) + (back[10], g_out, g_fgain, g_fgate, g_fup, g_down)
        carry = tuple((total + grad for total, grad in zip(carry, grads)))
        return (carry, (out_seq, dx_seq))
    shapes = (attn_gain,) + mats + params[:4] + (out_gain, w_out, ffn_gain, w_ffn_gate, w_ffn_up, w_ffn_down)
    init = tuple((jnp.zeros(array.shape, jnp.float32) for array in shapes))
    sums, (out_seqs, dx_seqs) = lax.scan(one_seq, init, (token_seqs, grad_seqs, seg_ids))
    block_out = out_seqs.reshape(seq_count * length, width)
    grad_tokens = dx_seqs.reshape(seq_count * length, width)
    return (block_out, grad_tokens, sums[0], sums[1], sums[2], sums[3], sums[4], sums[5], sums[6], sums[7], sums[8], sums[9], sums[10], sums[11], sums[12], sums[13], sums[14], sums[15], sums[16])
```

```python
from functools import partial
import math

import jax
import jax.numpy as jnp
from jax import lax
from jax.experimental import pallas as pl
from jax.experimental.pallas import tpu as pltpu
from jax.sharding import PartitionSpec as P

GROUP = 64


EPS_NORM = 1e-05
EPS_UNIT = 1e-06
HIGH = lax.Precision.HIGHEST
MID = lax.Precision.HIGH


def norm_gain(values, gain):
    return values * lax.rsqrt(jnp.mean(values * values, axis=-1, keepdims=True) + EPS_NORM) * gain


def shift_rows(values, offset, fill):
    padding = jnp.full((offset,) + values.shape[1:], fill, values.dtype)
    return jnp.concatenate([padding, values[:-offset]], axis=0)


def short_conv(values, taps, seg_row):
    total = taps[0] * values
    for offset in range(1, taps.shape[0]):
        keep = (seg_row == shift_rows(seg_row, offset, -1)).astype(values.dtype)
        total = total + taps[offset] * shift_rows(values, offset, 0) * keep[:, None]
    return total


def unit_rows(values):
    return values * lax.rsqrt(jnp.sum(values * values, axis=-1, keepdims=True) + EPS_UNIT)


def inverse_kernel(lower_ref, out_ref):
    count, size, _ = lower_ref.shape
    rows = lax.broadcasted_iota(jnp.int32, (size, size), 0)
    cols = lax.broadcasted_iota(jnp.int32, (size, size), 1)
    lowers = [lower_ref[i] for i in range(count)]
    eye = (rows == cols).astype(jnp.float32)
    pair = (rows // 2 == cols // 2).astype(jnp.float32)
    done = [eye - low * pair for low in lowers]
    half = 2
    while half < size:
        keep = (rows // (2 * half) == cols // (2 * half)) & (rows // half != cols // half)
        keep = keep.astype(jnp.float32)
        steps = [
            jnp.dot(low * keep, inv, precision=HIGH, preferred_element_type=jnp.float32)
            for low, inv in zip(lowers, done)
        ]
        done = [
            inv - jnp.dot(inv, step, precision=HIGH, preferred_element_type=jnp.float32)
            for inv, step in zip(done, steps)
        ]
        half *= 2
    for i in range(count):
        out_ref[i] = done[i]


@jax.custom_vjp
def unit_inverse(lower):
    return inverse_of(lower)


def inverse_of(lower):
    count, size, _ = lower.shape
    return pl.pallas_call(
        inverse_kernel,
        out_shape=jax.ShapeDtypeStruct(lower.shape, jnp.float32),
        in_specs=[pl.BlockSpec(memory_space=pltpu.VMEM)],
        out_specs=pl.BlockSpec(memory_space=pltpu.VMEM),
        cost_estimate=pl.CostEstimate(
            flops=120 * count * size**3, bytes_accessed=8 * count * size**2, transcendentals=0
        ),
        name="unit_inverse",
    )(lower)


def inverse_forward(lower):
    inv = inverse_of(lower)
    return inv, inv


def inverse_backward(inv, d_inv):
    left = jnp.einsum("bji,bjk->bik", inv, d_inv, precision=HIGH)
    return (-jnp.einsum("bik,blk->bil", left, inv, precision=HIGH),)


unit_inverse.defvjp(inverse_forward, inverse_backward)


def mixer(
    seg_row,
    q_proj,
    k_proj,
    v_proj,
    gate_proj,
    decay_proj,
    beta_proj,
    conv_query,
    conv_key,
    conv_value,
    decay_rate,
    out_gain,
):
    length = q_proj.shape[0]
    heads = decay_proj.shape[1]
    key_dim = q_proj.shape[1] // heads
    val_dim = v_proj.shape[1] // heads
    blocks = length // GROUP
    pairs = heads * blocks

    def by_head(array, dim):
        parts = [array[:, h * dim : (h + 1) * dim] for h in range(heads)]
        return jnp.stack(parts).reshape(pairs, GROUP, dim)

    query = unit_rows(by_head(jax.nn.silu(short_conv(q_proj, conv_query, seg_row)), key_dim))
    query = query / math.sqrt(key_dim)
    keys = unit_rows(by_head(jax.nn.silu(short_conv(k_proj, conv_key, seg_row)), key_dim))
    values = by_head(jax.nn.silu(short_conv(v_proj, conv_value, seg_row)), val_dim)
    beta = jax.nn.sigmoid(beta_proj).T.reshape(pairs, GROUP)
    log_decay = (-decay_rate[None, :] * jax.nn.softplus(decay_proj)).T.reshape(pairs, GROUP)

    index = jnp.arange(GROUP)
    lower = index[:, None] >= index[None, :]
    strict = (index[:, None] > index[None, :]).astype(jnp.float32)
    doc = seg_row.reshape(blocks, GROUP)
    prev_doc = jnp.concatenate([jnp.full((1,), -1, doc.dtype), doc[:-1, -1]])
    same_doc = ((doc[:, :, None] == doc[:, None, :]) & lower[None]).astype(jnp.float32)
    same_doc = jnp.tile(same_doc, (heads, 1, 1))
    from_prev = jnp.tile((doc == prev_doc[:, None]).astype(jnp.float32), (heads, 1))

    cum_log = jnp.sum(log_decay[:, None, :] * lower.astype(jnp.float32)[None], axis=2)
    spread = jnp.exp(jnp.minimum(cum_log[:, :, None] - cum_log[:, None, :], 0.0)) * same_doc
    carried = jnp.exp(cum_log) * from_prev
    mm = partial(jnp.einsum, precision=MID)
    key_key = mm("btd,bid->bti", keys, keys)
    inverse = unit_inverse(beta[:, :, None] * key_key * spread * strict[None])
    fresh = mm("bti,bid->btd", inverse, beta[:, :, None] * values)
    erased = mm("bti,bid->btd", inverse, (beta * carried)[:, :, None] * keys)
    late_keys = keys * spread[:, -1, :, None]
    add = mm("bid,bie->bde", late_keys, fresh)
    move = carried[:, -1][:, None, None] * jnp.eye(key_dim, dtype=jnp.float32)[None]
    move = move - mm("bid,bie->bde", late_keys, erased)
    add = add.reshape(heads, blocks, key_dim, val_dim)
    move = move.reshape(heads, blocks, key_dim, key_dim)
    state = jnp.zeros((heads, key_dim, val_dim), jnp.float32)
    states = [state]
    for n in range(blocks - 1):
        if n == 0:
            state = add[:, 0]
        else:
            state = mm("hij,hje->hie", move[:, n], state) + add[:, n]
        states.append(state)
    entering = jnp.stack(states, axis=1).reshape(pairs, key_dim, val_dim)
    delta = fresh - mm("btd,bde->bte", erased, entering)
    query_key = mm("btd,bid->bti", query, keys) * spread
    mixed = mm("bti,bie->bte", query_key, delta)
    mixed = mixed + mm("btd,bde->bte", query * carried[:, :, None], entering)
    normed = mixed * lax.rsqrt(jnp.mean(mixed * mixed, axis=-1, keepdims=True) + EPS_NORM)
    normed = (normed * out_gain).reshape(heads, length, val_dim)
    normed = jnp.concatenate([normed[h] for h in range(heads)], axis=1)
    return normed * jax.nn.silu(gate_proj)


def body(
    tokens,
    seg_ids,
    attn_gain,
    w_query,
    w_key,
    w_value,
    w_gate,
    w_decay,
    w_beta,
    conv_query,
    conv_key,
    conv_value,
    decay_rate,
    out_gain,
    w_out,
    ffn_gain,
    w_ffn_gate,
    w_ffn_up,
    w_ffn_down,
    grad_out,
):
    seg_row = seg_ids[0]
    mats = (w_query, w_key, w_value, w_gate, w_decay, w_beta)
    x_float = tokens.astype(jnp.float32)
    xnorm_rows = norm_gain(x_float, attn_gain).astype(jnp.bfloat16)
    width = tokens.shape[1]
    both = lax.all_gather(
        jnp.concatenate([xnorm_rows, grad_out], axis=1), "tensor", axis=0, tiled=True
    )
    xnorm, grad_full = both[:, :width], both[:, width:]
    mats_cat = jnp.concatenate(mats, axis=1)
    cuts = []
    for weight in mats[:-1]:
        cuts.append(weight.shape[1] + (cuts[-1] if cuts else 0))
    projs = jnp.split(
        jnp.dot(xnorm, mats_cat, preferred_element_type=jnp.float32), cuts, axis=1
    )
    mixed, pull_mix = jax.vjp(
        partial(mixer, seg_row),
        projs[0],
        projs[1],
        projs[2],
        projs[3],
        projs[4],
        projs[5],
        conv_query,
        conv_key,
        conv_value,
        decay_rate,
        out_gain,
    )
    gated = mixed.astype(jnp.bfloat16)
    rows_part = gated
    resid = x_float + lax.psum_scatter(
        jnp.dot(rows_part, w_out, preferred_element_type=jnp.float32),
        "tensor",
        scatter_dimension=0,
        tiled=True,
    )
    hnorm_rows = norm_gain(resid, ffn_gain).astype(jnp.bfloat16)
    hnorm = lax.all_gather(hnorm_rows, "tensor", axis=0, tiled=True)
    up_in = jnp.dot(hnorm, w_ffn_gate, preferred_element_type=jnp.float32)
    up_val = jnp.dot(hnorm, w_ffn_up, preferred_element_type=jnp.float32)
    act = (jax.nn.silu(up_in) * up_val).astype(jnp.bfloat16)
    rows_part = act
    block_out = (
        resid
        + lax.psum_scatter(
            jnp.dot(rows_part, w_ffn_down, preferred_element_type=jnp.float32).astype(jnp.bfloat16),
            "tensor",
            scatter_dimension=0,
            tiled=True,
        ).astype(jnp.float32)
    ).astype(jnp.bfloat16)
    d_act = jnp.einsum("td,fd->tf", grad_full, w_ffn_down, preferred_element_type=jnp.float32)
    g_down = jnp.einsum("td,tf->df", grad_full, act, preferred_element_type=jnp.float32)
    gate_sig = jax.nn.sigmoid(up_in)
    d_up_in = (d_act * up_val * gate_sig * (1.0 + up_in * (1.0 - gate_sig))).astype(jnp.bfloat16)
    d_up_val = (d_act * up_in * gate_sig).astype(jnp.bfloat16)
    g_fgate = jnp.einsum("td,tf->df", hnorm, d_up_in, preferred_element_type=jnp.float32)
    g_fup = jnp.einsum("td,tf->df", hnorm, d_up_val, preferred_element_type=jnp.float32)
    total = jnp.einsum("tf,df->td", d_up_in, w_ffn_gate, preferred_element_type=jnp.float32)
    d_hnorm = lax.psum_scatter(
        (
            total + jnp.einsum("tf,df->td", d_up_val, w_ffn_up, preferred_element_type=jnp.float32)
        ).astype(jnp.bfloat16),
        "tensor",
        scatter_dimension=0,
        tiled=True,
    ).astype(jnp.float32)
    _, pull_mid = jax.vjp(norm_gain, resid, ffn_gain)
    d_resid_norm, g_fgain = pull_mid(d_hnorm)
    d_resid = grad_out.astype(jnp.float32) + d_resid_norm
    d_resid_full = lax.all_gather(d_resid.astype(jnp.bfloat16), "tensor", axis=0, tiled=True)
    g_out = jnp.einsum("td,tc->dc", d_resid_full, gated, preferred_element_type=jnp.float32)
    d_gated = jnp.einsum("td,cd->tc", d_resid_full, w_out, preferred_element_type=jnp.float32)
    back = pull_mix(d_gated)
    d_projs = [grad.astype(jnp.bfloat16) for grad in back[:6]]

    def sum_rows(parts):
        joined = jnp.concatenate([part.astype(jnp.bfloat16) for part in parts], axis=1)
        out = lax.psum_scatter(joined, "dp", scatter_dimension=0, tiled=True)
        edges = []
        for part in parts[:-1]:
            edges.append(part.shape[1] + (edges[-1] if edges else 0))
        return jnp.split(out.astype(jnp.float32), edges, axis=1)

    g_gate = jnp.einsum("td,tc->dc", xnorm, d_projs[3], preferred_element_type=jnp.float32)
    s_fgate, s_fup, s_down, s_out, s_gate = sum_rows((g_fgate, g_fup, g_down, g_out, g_gate))
    d_cat = jnp.concatenate(d_projs, axis=1)
    total = jnp.einsum("tc,dc->td", d_cat, mats_cat, preferred_element_type=jnp.float32)
    d_xnorm = lax.psum_scatter(
        total.astype(jnp.bfloat16), "tensor", scatter_dimension=0, tiled=True
    ).astype(jnp.float32)
    g_again = jnp.sum(total * (xnorm.astype(jnp.float32) / attn_gain), axis=0)
    _, pull_first = jax.vjp(lambda rows: norm_gain(rows, attn_gain), x_float)
    (d_x_norm,) = pull_first(d_xnorm)
    grad_tokens = (d_resid + d_x_norm).astype(jnp.bfloat16)
    rest = [d_projs[0], d_projs[1], d_projs[2], d_projs[4], d_projs[5]]
    g_rest = jnp.einsum(
        "td,tc->dc", xnorm, jnp.concatenate(rest, axis=1), preferred_element_type=jnp.float32
    ).astype(jnp.bfloat16)
    s_rest = lax.psum_scatter(g_rest, "dp", scatter_dimension=0, tiled=True).astype(jnp.float32)
    edges = []
    for part in rest[:-1]:
        edges.append(part.shape[1] + (edges[-1] if edges else 0))
    s_query, s_key, s_value, s_decay, s_beta = jnp.split(s_rest, edges, axis=1)
    weight_sums = (
        s_query, s_key, s_value, s_gate, s_decay, s_beta, s_out.T, s_fgate, s_fup, s_down.T
    )
    rate_parts = lax.psum((back[6], back[7], back[8], back[9]), "dp")
    gain_parts = lax.psum((g_again, g_fgain, back[10]), ("dp", "tensor"))
    return (
        block_out,
        grad_tokens,
        gain_parts[0],
        weight_sums[0],
        weight_sums[1],
        weight_sums[2],
        weight_sums[3],
        weight_sums[4],
        weight_sums[5],
        rate_parts[0],
        rate_parts[1],
        rate_parts[2],
        rate_parts[3],
        gain_parts[2],
        weight_sums[6],
        gain_parts[1],
        weight_sums[7],
        weight_sums[8],
        weight_sums[9],
    )


def solution(mesh):
    in_specs = (
        P(("dp", "tensor"), None),
        P("dp", None),
        P(),
        P(None, "tensor"),
        P(None, "tensor"),
        P(None, "tensor"),
        P(None, "tensor"),
        P(None, "tensor"),
        P(None, "tensor"),
        P(None, "tensor"),
        P(None, "tensor"),
        P(None, "tensor"),
        P("tensor"),
        P(),
        P("tensor", None),
        P(),
        P(None, "tensor"),
        P(None, "tensor"),
        P("tensor", None),
        P(("dp", "tensor"), None),
    )
    out_specs = (
        P(("dp", "tensor"), None),
        P(("dp", "tensor"), None),
        P(),
        P("dp", "tensor"),
        P("dp", "tensor"),
        P("dp", "tensor"),
        P("dp", "tensor"),
        P("dp", "tensor"),
        P("dp", "tensor"),
        P(None, "tensor"),
        P(None, "tensor"),
        P(None, "tensor"),
        P("tensor"),
        P(),
        P("tensor", "dp"),
        P(),
        P("dp", "tensor"),
        P("dp", "tensor"),
        P("tensor", "dp"),
    )
    return jax.shard_map(body, mesh=mesh, in_specs=in_specs, out_specs=out_specs, check_vma=False)
```

```python
from functools import partial
import math

import jax
import jax.numpy as jnp
from jax import lax
from jax.experimental import pallas as pl
from jax.experimental.pallas import tpu as pltpu
from jax.sharding import PartitionSpec as P

GROUP = 64
LANES = 128


EPS_NORM = 1e-05
EPS_UNIT = 1e-06
HIGH = lax.Precision.HIGHEST
MID = lax.Precision.HIGH


def norm_gain(values, gain):
    return values * lax.rsqrt(jnp.mean(values * values, axis=-1, keepdims=True) + EPS_NORM) * gain


def shift_rows(values, offset, fill):
    padding = jnp.full((offset,) + values.shape[1:], fill, values.dtype)
    return jnp.concatenate([padding, values[:-offset]], axis=0)


def short_conv(values, taps, seg_row):
    total = taps[0] * values
    for offset in range(1, taps.shape[0]):
        keep = (seg_row == shift_rows(seg_row, offset, -1)).astype(values.dtype)
        total = total + taps[offset] * shift_rows(values, offset, 0) * keep[:, None]
    return total


def unit_rows(values):
    return values * lax.rsqrt(jnp.sum(values * values, axis=-1, keepdims=True) + EPS_UNIT)


def inverse_kernel(lower_ref, out_ref):
    count, size, _ = lower_ref.shape
    rows = lax.broadcasted_iota(jnp.int32, (size, size), 0)
    cols = lax.broadcasted_iota(jnp.int32, (size, size), 1)
    lowers = [lower_ref[i] for i in range(count)]
    eye = (rows == cols).astype(jnp.float32)
    pair = (rows // 2 == cols // 2).astype(jnp.float32)
    done = [eye - low * pair for low in lowers]
    half = 2
    while half < size:
        keep = (rows // (2 * half) == cols // (2 * half)) & (rows // half != cols // half)
        keep = keep.astype(jnp.float32)
        steps = [
            jnp.dot(low * keep, inv, precision=HIGH, preferred_element_type=jnp.float32)
            for low, inv in zip(lowers, done)
        ]
        done = [
            inv - jnp.dot(inv, step, precision=HIGH, preferred_element_type=jnp.float32)
            for inv, step in zip(done, steps)
        ]
        half *= 2
    for i in range(count):
        out_ref[i] = done[i]


@jax.custom_vjp
def unit_inverse(lower):
    return inverse_of(lower)


def inverse_of(lower):
    count, size, _ = lower.shape
    return pl.pallas_call(
        inverse_kernel,
        out_shape=jax.ShapeDtypeStruct(lower.shape, jnp.float32),
        in_specs=[pl.BlockSpec(memory_space=pltpu.VMEM)],
        out_specs=pl.BlockSpec(memory_space=pltpu.VMEM),
        cost_estimate=pl.CostEstimate(
            flops=120 * count * size**3, bytes_accessed=8 * count * size**2, transcendentals=0
        ),
        name="unit_inverse",
    )(lower)


def inverse_forward(lower):
    inv = inverse_of(lower)
    return inv, inv


def inverse_backward(inv, d_inv):
    left = jnp.einsum("bji,bjk->bik", inv, d_inv, precision=HIGH)
    return (-jnp.einsum("bik,blk->bil", left, inv, precision=HIGH),)


unit_inverse.defvjp(inverse_forward, inverse_backward)


def mixer(
    seg_row,
    q_proj,
    k_proj,
    v_proj,
    decay_proj,
    beta_proj,
    conv_query,
    conv_key,
    conv_value,
    decay_rate,
    out_gain,
):
    length = q_proj.shape[0]
    heads = decay_proj.shape[1]
    key_dim = q_proj.shape[1] // heads
    val_dim = v_proj.shape[1] // heads
    blocks = length // GROUP
    pairs = heads * blocks

    def by_head(array, dim):
        parts = [array[:, h * dim : (h + 1) * dim] for h in range(heads)]
        return jnp.stack(parts).reshape(pairs, GROUP, dim)

    query = unit_rows(by_head(jax.nn.silu(short_conv(q_proj, conv_query, seg_row)), key_dim))
    query = query / math.sqrt(key_dim)
    keys = unit_rows(by_head(jax.nn.silu(short_conv(k_proj, conv_key, seg_row)), key_dim))
    values = by_head(jax.nn.silu(short_conv(v_proj, conv_value, seg_row)), val_dim)
    beta = jax.nn.sigmoid(beta_proj).T.reshape(pairs, GROUP)
    log_decay = (-decay_rate[None, :] * jax.nn.softplus(decay_proj)).T.reshape(pairs, GROUP)

    index = jnp.arange(GROUP)
    lower = index[:, None] >= index[None, :]
    strict = (index[:, None] > index[None, :]).astype(jnp.float32)
    doc = seg_row.reshape(blocks, GROUP)
    prev_doc = jnp.concatenate([jnp.full((1,), -1, doc.dtype), doc[:-1, -1]])
    same_doc = ((doc[:, :, None] == doc[:, None, :]) & lower[None]).astype(jnp.float32)
    same_doc = jnp.tile(same_doc, (heads, 1, 1))
    from_prev = jnp.tile((doc == prev_doc[:, None]).astype(jnp.float32), (heads, 1))

    cum_log = jnp.sum(log_decay[:, None, :] * lower.astype(jnp.float32)[None], axis=2)
    spread = jnp.exp(jnp.minimum(cum_log[:, :, None] - cum_log[:, None, :], 0.0)) * same_doc
    carried = jnp.exp(cum_log) * from_prev
    mm = partial(jnp.einsum, precision=MID)
    key_key = mm("btd,bid->bti", keys, keys)
    inverse = unit_inverse(beta[:, :, None] * key_key * spread * strict[None])
    fresh = mm("bti,bid->btd", inverse, beta[:, :, None] * values)
    erased = mm("bti,bid->btd", inverse, (beta * carried)[:, :, None] * keys)
    late_keys = keys * spread[:, -1, :, None]
    add = mm("bid,bie->bde", late_keys, fresh)
    move = carried[:, -1][:, None, None] * jnp.eye(key_dim, dtype=jnp.float32)[None]
    move = move - mm("bid,bie->bde", late_keys, erased)
    add = add.reshape(heads, blocks, key_dim, val_dim)
    move = move.reshape(heads, blocks, key_dim, key_dim)
    state = jnp.zeros((heads, key_dim, val_dim), jnp.float32)
    states = [state]
    for n in range(blocks - 1):
        if n == 0:
            state = add[:, 0]
        else:
            state = mm("hij,hje->hie", move[:, n], state) + add[:, n]
        states.append(state)
    entering = jnp.stack(states, axis=1).reshape(pairs, key_dim, val_dim)
    delta = fresh - mm("btd,bde->bte", erased, entering)
    query_key = mm("btd,bid->bti", query, keys) * spread
    mixed = mm("bti,bie->bte", query_key, delta)
    mixed = mixed + mm("btd,bde->bte", query * carried[:, :, None], entering)
    normed = mixed * lax.rsqrt(jnp.mean(mixed * mixed, axis=-1, keepdims=True) + EPS_NORM)
    normed = (normed * out_gain).reshape(heads, length, val_dim)
    normed = jnp.concatenate([normed[h] for h in range(heads)], axis=1)
    return normed


def pad_lanes(part):
    return jnp.pad(part, ((0, 0), (0, -part.shape[1] % LANES)))


def cut_lanes(joined, parts):
    out, edge = [], 0
    for part in parts:
        columns = part.shape[1]
        out.append(joined[:, edge : edge + columns].astype(jnp.float32))
        edge += columns + (-columns % LANES)
    return out


def body(
    tokens,
    seg_ids,
    attn_gain,
    w_query,
    w_key,
    w_value,
    w_gate,
    w_decay,
    w_beta,
    conv_query,
    conv_key,
    conv_value,
    decay_rate,
    out_gain,
    w_out,
    ffn_gain,
    w_ffn_gate,
    w_ffn_up,
    w_ffn_down,
    grad_out,
):
    seg_row = seg_ids[0]
    mats = (w_query, w_key, w_value, w_gate, w_decay, w_beta)
    x_float = tokens.astype(jnp.float32)
    xnorm_rows = norm_gain(x_float, attn_gain).astype(jnp.bfloat16)
    xnorm_rows, mats = lax.optimization_barrier((xnorm_rows, mats))
    xnorm = lax.all_gather(xnorm_rows, "tensor", axis=0, tiled=True)
    grad_full = lax.all_gather(grad_out, "tensor", axis=0, tiled=True)
    mats_cat = jnp.concatenate(mats, axis=1)
    cuts = []
    for weight in mats[:-1]:
        cuts.append(weight.shape[1] + (cuts[-1] if cuts else 0))
    projs = jnp.split(
        jnp.dot(xnorm, mats_cat, preferred_element_type=jnp.float32), cuts, axis=1
    )
    normed, pull_mix = jax.vjp(
        partial(mixer, seg_row),
        projs[0],
        projs[1],
        projs[2],
        projs[4],
        projs[5],
        conv_query,
        conv_key,
        conv_value,
        decay_rate,
        out_gain,
    )
    mixed, pull_gate = jax.vjp(lambda rows, gate: rows * jax.nn.silu(gate), normed, projs[3])
    gated, grad_full = lax.optimization_barrier((mixed.astype(jnp.bfloat16), grad_full))
    rows_part = gated
    resid = x_float + lax.psum_scatter(
        jnp.dot(rows_part, w_out, preferred_element_type=jnp.float32).astype(jnp.bfloat16),
        "tensor",
        scatter_dimension=0,
        tiled=True,
    ).astype(jnp.float32)
    hnorm_rows = norm_gain(resid, ffn_gain).astype(jnp.bfloat16)
    hnorm = lax.all_gather(hnorm_rows, "tensor", axis=0, tiled=True)
    up_in = jnp.dot(hnorm, w_ffn_gate, preferred_element_type=jnp.float32)
    up_val = jnp.dot(hnorm, w_ffn_up, preferred_element_type=jnp.float32)
    act = (jax.nn.silu(up_in) * up_val).astype(jnp.bfloat16)
    rows_part = act
    ffn_rows = lax.psum_scatter(
        jnp.dot(rows_part, w_ffn_down, preferred_element_type=jnp.float32).astype(jnp.bfloat16),
        "tensor",
        scatter_dimension=0,
        tiled=True,
    )
    d_act = jnp.einsum("td,fd->tf", grad_full, w_ffn_down, preferred_element_type=jnp.float32)
    g_down = jnp.einsum("td,tf->df", grad_full, act, preferred_element_type=jnp.float32)
    gate_sig = jax.nn.sigmoid(up_in)
    d_up_in = (d_act * up_val * gate_sig * (1.0 + up_in * (1.0 - gate_sig))).astype(jnp.bfloat16)
    d_up_val = (d_act * up_in * gate_sig).astype(jnp.bfloat16)
    g_fgate = jnp.einsum("td,tf->df", hnorm, d_up_in, preferred_element_type=jnp.float32)
    g_fup = jnp.einsum("td,tf->df", hnorm, d_up_val, preferred_element_type=jnp.float32)
    total = jnp.einsum("tf,df->td", d_up_in, w_ffn_gate, preferred_element_type=jnp.float32)
    d_hnorm = lax.psum_scatter(
        (
            total + jnp.einsum("tf,df->td", d_up_val, w_ffn_up, preferred_element_type=jnp.float32)
        ).astype(jnp.bfloat16),
        "tensor",
        scatter_dimension=0,
        tiled=True,
    ).astype(jnp.float32)
    _, pull_mid = jax.vjp(norm_gain, resid, ffn_gain)
    d_resid_norm, g_fgain = pull_mid(d_hnorm)
    d_resid = grad_out.astype(jnp.float32) + d_resid_norm
    d_resid_full = lax.all_gather(d_resid.astype(jnp.bfloat16), "tensor", axis=0, tiled=True)
    g_out = jnp.einsum("td,tc->dc", d_resid_full, gated, preferred_element_type=jnp.float32)
    d_gated = jnp.einsum("td,cd->tc", d_resid_full, w_out, preferred_element_type=jnp.float32)
    d_normed, d_gate = pull_gate(d_gated)
    d_gate = d_gate.astype(jnp.bfloat16)
    g_gate = jnp.einsum("td,tc->dc", xnorm, d_gate, preferred_element_type=jnp.float32)
    first = (g_fgate, g_fup, g_down, g_out, g_gate)
    joined = jnp.concatenate([pad_lanes(part.astype(jnp.bfloat16)) for part in first], axis=1)
    d_normed, joined = lax.optimization_barrier((d_normed, joined))
    s_first = lax.psum_scatter(joined, "dp", scatter_dimension=0, tiled=True)
    back = pull_mix(d_normed)
    back, s_first, ffn_rows = lax.optimization_barrier((back, s_first, ffn_rows))
    block_out = (resid + ffn_rows.astype(jnp.float32)).astype(jnp.bfloat16)
    s_fgate, s_fup, s_down, s_out, s_gate = cut_lanes(s_first, first)
    d_projs = [grad.astype(jnp.bfloat16) for grad in back[:5]]
    d_projs.insert(3, d_gate)
    d_cat = jnp.concatenate(d_projs, axis=1)
    total = jnp.einsum("tc,dc->td", d_cat, mats_cat, preferred_element_type=jnp.float32)
    d_xnorm = lax.psum_scatter(
        total.astype(jnp.bfloat16), "tensor", scatter_dimension=0, tiled=True
    ).astype(jnp.float32)
    g_again = jnp.sum(total * (xnorm.astype(jnp.float32) / attn_gain), axis=0)
    _, pull_first = jax.vjp(lambda rows: norm_gain(rows, attn_gain), x_float)
    (d_x_norm,) = pull_first(d_xnorm)
    grad_tokens = (d_resid + d_x_norm).astype(jnp.bfloat16)
    rest = [d_projs[0], d_projs[1], d_projs[2], d_projs[4], d_projs[5]]
    g_rest = jnp.einsum(
        "td,tc->dc", xnorm, jnp.concatenate(rest, axis=1), preferred_element_type=jnp.float32
    ).astype(jnp.bfloat16)
    s_rest = lax.psum_scatter(g_rest, "dp", scatter_dimension=0, tiled=True).astype(jnp.float32)
    edges = []
    for part in rest[:-1]:
        edges.append(part.shape[1] + (edges[-1] if edges else 0))
    s_query, s_key, s_value, s_decay, s_beta = jnp.split(s_rest, edges, axis=1)
    weight_sums = (
        s_query, s_key, s_value, s_gate, s_decay, s_beta, s_out.T, s_fgate, s_fup, s_down.T
    )
    rate_parts = lax.psum((back[5], back[6], back[7], back[8]), "dp")
    gain_parts = lax.psum((g_again, g_fgain, back[9]), ("dp", "tensor"))
    return (
        block_out,
        grad_tokens,
        gain_parts[0],
        weight_sums[0],
        weight_sums[1],
        weight_sums[2],
        weight_sums[3],
        weight_sums[4],
        weight_sums[5],
        rate_parts[0],
        rate_parts[1],
        rate_parts[2],
        rate_parts[3],
        gain_parts[2],
        weight_sums[6],
        gain_parts[1],
        weight_sums[7],
        weight_sums[8],
        weight_sums[9],
    )


def solution(mesh):
    in_specs = (
        P(("dp", "tensor"), None),
        P("dp", None),
        P(),
        P(None, "tensor"),
        P(None, "tensor"),
        P(None, "tensor"),
        P(None, "tensor"),
        P(None, "tensor"),
        P(None, "tensor"),
        P(None, "tensor"),
        P(None, "tensor"),
        P(None, "tensor"),
        P("tensor"),
        P(),
        P("tensor", None),
        P(),
        P(None, "tensor"),
        P(None, "tensor"),
        P("tensor", None),
        P(("dp", "tensor"), None),
    )
    out_specs = (
        P(("dp", "tensor"), None),
        P(("dp", "tensor"), None),
        P(),
        P("dp", "tensor"),
        P("dp", "tensor"),
        P("dp", "tensor"),
        P("dp", "tensor"),
        P("dp", "tensor"),
        P("dp", "tensor"),
        P(None, "tensor"),
        P(None, "tensor"),
        P(None, "tensor"),
        P("tensor"),
        P(),
        P("tensor", "dp"),
        P(),
        P("dp", "tensor"),
        P("dp", "tensor"),
        P("tensor", "dp"),
    )
    return jax.shard_map(body, mesh=mesh, in_specs=in_specs, out_specs=out_specs, check_vma=False)
```
